32 devices in a mesh: ha: 8 (over z, x), ta: 4 (over y, core).
Axes of the slice: x: 2, y: 2, z: 4, core: 2. Of those that a mesh axis runs over, the one named last changes fastest.
Arguments:
- layer_input: bfloat16 [8, 24, 192, 128], P('ta', 'ha'), may hold values from -6 to 6
- pre_one: bfloat16 [8, 24, 192, 128], P('ta', 'ha'), may hold values from -9 to 9
- pre_two: bfloat16 [8, 24, 192, 128], P('ta', 'ha'), may hold values from -9 to 9
- pre_three: bfloat16 [8, 24, 192, 128], P('ta', 'ha'), may hold values from -9 to 9
- kernel_one: bfloat16 [3, 3, 3, 128, 128], replicated, may hold values from -0.109375 to 0.109375
- kernel_two: bfloat16 [3, 3, 3, 128, 128], replicated, may hold values from -0.109375 to 0.109375
- kernel_three: bfloat16 [3, 3, 3, 128, 128], replicated, may hold values from -0.109375 to 0.109375
- upstream: bfloat16 [8, 24, 192, 128], P('ta', 'ha'), may hold values from -24 to 24
Outputs:
- input_gradient: bfloat16 [8, 24, 192, 128], P('ta', 'ha')
- kernel_grad_one: float32 [3, 3, 3, 128, 128], P(None, None, None, 'ha')
- kernel_grad_two: float32 [3, 3, 3, 128, 128], P(None, None, None, 'ha')
- kernel_grad_three: float32 [3, 3, 3, 128, 128], P(None, None, None, 'ha')
The draws below stay inside these ranges and needn't reach their ends.
All inputs are finite; a program needn't handle non-finite values.
Results may differ from the reference program's by a relative error of at most 0.014.
Values may be sent and summed in bfloat16 or wider, within the bound.
A program may use at most 128 MiB of HBM per device.

```python
import math
import jax
import jax.numpy as jnp
from jax import lax

C = 128
W = 192
F = 8
H = 24


def level_of(key, dims, cuts, smallest, largest):
    loudness = 1.0
    for position, shards_of in cuts:
        heights = jax.random.uniform(jax.random.fold_in(jax.random.fold_in(key, 6), position), (shards_of,), jnp.float32, smallest / len(cuts), largest / len(cuts))
        loudness = loudness * jnp.repeat(jnp.exp(heights), dims[position] // shards_of).reshape((-1,) + (1,) * (len(dims) - 1 - position))
    return loudness


def noise(key, shape, scale, reach, pieces=(), kind=jnp.bfloat16):
    result = scale * jax.random.normal(key, shape, jnp.float32)
    if pieces:
        result = result * level_of(key, shape, pieces, -0.22, 0.18)
    return jnp.clip(result, -reach, reach).astype(kind)


def setup_inputs(seed: int = 0) -> dict:
    streams_of = jax.random.split(jax.random.key(seed), 9)
    layer_input = noise(streams_of[0], (F, H, W, C), 1.0, 6.0, ((0, 4), (1, 8)))
    pre_one = noise(streams_of[1], (F, H, W, C), 1.5, 9.0, ((0, 4), (1, 8)))
    pre_two = noise(streams_of[2], (F, H, W, C), 1.5, 9.0, ((0, 4), (1, 8)))
    pre_three = noise(streams_of[3], (F, H, W, C), 1.5, 9.0, ((0, 4), (1, 8)))
    kernel_one = noise(streams_of[4], (3, 3, 3, C, C), (27 * C) ** -0.5, 0.109375)
    kernel_two = noise(streams_of[5], (3, 3, 3, C, C), (27 * C) ** -0.5, 0.109375)
    kernel_three = noise(streams_of[6], (3, 3, 3, C, C), (27 * C) ** -0.5, 0.109375)
    upstream = noise(streams_of[7], (F, H, W, C), 4.0, 24.0, ((0, 4), (1, 8)))
    return {"layer_input": layer_input, "pre_one": pre_one, "pre_two": pre_two, "pre_three": pre_three, "kernel_one": kernel_one, "kernel_two": kernel_two, "kernel_three": kernel_three, "upstream": upstream}


def silu_slope(pre_values):
    values = pre_values.astype(jnp.float32)
    sigmoid = jax.nn.sigmoid(values)
    return sigmoid * (1.0 + values * (1.0 - sigmoid))

def kernel_grad(inputs, gradient):
    padded = jnp.pad(inputs, ((2, 0), (1, 1), (1, 1), (0, 0)))
    norm_scale = 1.0 / math.sqrt(F * H * W)

    def step(running, frame_index):
        window = lax.dynamic_slice_in_dim(padded, frame_index, 3, 0)
        tap_list = [window[tap_time, tap_row:tap_row + H, tap_col:tap_col + W] for tap_time in range(3) for tap_row in range(3) for tap_col in range(3)]
        patches = jnp.concatenate(tap_list, -1).reshape(H * W, 27 * C)
        current = lax.dynamic_index_in_dim(gradient, frame_index, 0, keepdims=False).reshape(H * W, C)
        contribution = lax.dot_general(patches, current, (((0,), (0,)), ((), ())), preferred_element_type=jnp.float32)
        return (running + contribution, None)
    running, _ = lax.scan(step, jnp.zeros((27 * C, C), jnp.float32), jnp.arange(F, dtype=jnp.int32))
    return (running * norm_scale).reshape(3, 3, 3, C, C)

def input_grad(gradient, kernel):
    padded = jnp.pad(gradient, ((0, 2), (1, 1), (1, 1), (0, 0)))
    flipped = jnp.swapaxes(kernel, 3, 4).reshape(27 * C, C)

    def frame_result(frame_index):
        window = lax.dynamic_slice_in_dim(padded, frame_index, 3, 0)
        tap_list = [window[2 - tap_time, 2 - tap_row:2 - tap_row + H, 2 - tap_col:2 - tap_col + W] for tap_time in range(3) for tap_row in range(3) for tap_col in range(3)]
        patches = jnp.concatenate(tap_list, -1).reshape(H * W, 27 * C)
        return jnp.dot(patches, flipped, preferred_element_type=jnp.float32)
    return lax.map(frame_result, jnp.arange(F, dtype=jnp.int32)).reshape(F, H, W, C)

def reference(layer_input, pre_one, pre_two, pre_three, kernel_one, kernel_two, kernel_three, upstream):
    act_one = jax.nn.silu(pre_one.astype(jnp.float32)).astype(jnp.bfloat16)
    act_two = jax.nn.silu(pre_two.astype(jnp.float32)).astype(jnp.bfloat16)
    grad_three = (upstream.astype(jnp.float32) * silu_slope(pre_three)).astype(jnp.bfloat16)
    kernel_grad_three = kernel_grad(act_two, grad_three)
    grad_two = (input_grad(grad_three, kernel_three) * silu_slope(pre_two)).astype(jnp.bfloat16)
    kernel_grad_two = kernel_grad(act_one, grad_two)
    grad_one = (input_grad(grad_two, kernel_two) * silu_slope(pre_one)).astype(jnp.bfloat16)
    kernel_grad_one = kernel_grad(layer_input, grad_one)
    input_gradient = input_grad(grad_one, kernel_one).astype(jnp.bfloat16)
    return (input_gradient, kernel_grad_one, kernel_grad_two, kernel_grad_three)
```

```python
import functools
import math

import jax
import jax.numpy as jnp
from jax import lax
from jax.experimental import pallas as pl
from jax.experimental.pallas import tpu as pltpu
from jax.sharding import PartitionSpec as P

MESH = pl.DeviceIdType.MESH
VMEM = pl.BlockSpec(memory_space=pltpu.VMEM)


def silu_slope(pre_values):
    values = pre_values.astype(jnp.float32)
    sigmoid = jax.nn.sigmoid(values)
    return sigmoid * (1.0 + values * (1.0 - sigmoid))


def exchange(ta_n, ha_n, g_ref, out_ref, send_sems, recv_sems):
    ta, ha = lax.axis_index("ta"), lax.axis_index("ha")
    frames, rows = g_ref.shape[0], g_ref.shape[1]
    has_up, has_down = ha > 0, ha < ha_n - 1
    has_earlier, has_later = ta > 0, ta < ta_n - 1
    barrier = pltpu.get_barrier_semaphore()

    def device(d_ta, d_ha):
        return (ha + d_ha, ta + d_ta)

    def copy(index, source, target, d_ta, d_ha):
        return pltpu.make_async_remote_copy(
            src_ref=source,
            dst_ref=target,
            send_sem=send_sems.at[index],
            recv_sem=recv_sems.at[index],
            device_id=device(d_ta, d_ha),
            device_id_type=MESH,
        )

    for there, d_ta, d_ha in ((has_up, 0, -1), (has_down, 0, 1), (has_later, 1, 0)):

        @pl.when(there)
        def _():
            pl.semaphore_signal(barrier, inc=1, device_id=device(d_ta, d_ha), device_id_type=MESH)

    below = copy(0, g_ref.at[:, rows - 1], out_ref.at[pl.ds(0, frames), 0], 0, 1)
    above = copy(1, g_ref.at[:, 0], out_ref.at[pl.ds(0, frames), rows + 1], 0, -1)
    earlier = copy(2, g_ref, out_ref.at[pl.ds(frames, 2), pl.ds(1, rows)], -1, 0)
    corner_top = copy(3, out_ref.at[pl.ds(0, frames), 0], out_ref.at[pl.ds(frames, 2), 0], -1, 0)
    corner_end = copy(
        4, out_ref.at[pl.ds(0, frames), rows + 1], out_ref.at[pl.ds(frames, 2), rows + 1], -1, 0
    )
    peers = has_up.astype(jnp.int32) + has_down.astype(jnp.int32) + has_earlier.astype(jnp.int32)
    pl.semaphore_wait(barrier, peers)
    pl.when(has_down)(below.start)
    pl.when(has_up)(above.start)
    pl.when(has_earlier)(earlier.start)
    zero_row = jnp.zeros((frames,) + g_ref.shape[2:], g_ref.dtype)

    @pl.when(jnp.logical_not(has_up))
    def _():
        out_ref[0:frames, 0] = zero_row
        out_ref[frames : frames + 2, 0] = zero_row

    @pl.when(jnp.logical_not(has_down))
    def _():
        out_ref[0:frames, rows + 1] = zero_row
        out_ref[frames : frames + 2, rows + 1] = zero_row

    @pl.when(jnp.logical_not(has_later))
    def _():
        for row in range(rows + 2):
            out_ref[frames : frames + 2, row] = zero_row

    out_ref[0:frames, 1 : rows + 1] = g_ref[...]

    @pl.when(has_up)
    def _():
        below.wait_recv()

        @pl.when(has_earlier)
        def _():
            corner_top.start()

    @pl.when(has_down)
    def _():
        above.wait_recv()

        @pl.when(has_earlier)
        def _():
            corner_end.start()

    @pl.when(has_later)
    def _():
        earlier.wait_recv()
        pl.when(has_up)(corner_top.wait_recv)
        pl.when(has_down)(corner_end.wait_recv)

    pl.when(has_down)(below.wait_send)
    pl.when(has_up)(above.wait_send)

    @pl.when(has_earlier)
    def _():
        earlier.wait_send()
        pl.when(has_up)(corner_top.wait_send)
        pl.when(has_down)(corner_end.wait_send)


def halo(gradient, ta_n, ha_n):
    frames, rows, cols, channels = gradient.shape
    return pl.pallas_call(
        functools.partial(exchange, ta_n, ha_n),
        out_shape=jax.ShapeDtypeStruct((frames + 2, rows + 2, cols, channels), gradient.dtype),
        in_specs=[VMEM],
        out_specs=VMEM,
        scratch_shapes=[pltpu.SemaphoreType.DMA((5,)), pltpu.SemaphoreType.DMA((5,))],
        compiler_params=pltpu.CompilerParams(collective_id=0, has_side_effects=True),
        name="halo",
    )(gradient)


def convolve(last, act, wide_ref, x_ref, pre_ref, k_ref, kg_ref, out_ref, shifted):
    frames, rows, cols, channels = x_ref.shape
    column = lax.broadcasted_iota(jnp.int32, (cols, channels), 0)
    for f in range(frames + 2):
        for r in range(rows + 2):
            line = wide_ref[f, r]
            wide = line.astype(jnp.float32)
            after = jnp.where(column < cols - 1, pltpu.roll(wide, cols - 1, 0), 0.0)
            before = jnp.where(column > 0, pltpu.roll(wide, 1, 0), 0.0)
            shifted[f, r, :, 0:channels] = after.astype(line.dtype)
            shifted[f, r, :, channels : 2 * channels] = line
            shifted[f, r, :, 2 * channels : 3 * channels] = before.astype(line.dtype)

    def window(f, a, b):
        return shifted[f + 2 - a, 2 - b : 2 - b + rows].reshape(rows * cols, 3 * channels)

    taps = [(a, b) for a in range(3) for b in range(3)]
    inputs = []
    for f in range(frames):
        values = x_ref[f].reshape(rows * cols, channels)
        if act:
            wide = values.astype(jnp.float32)
            values = (wide * jax.nn.sigmoid(wide)).astype(jnp.bfloat16)
        inputs.append(values.T)
    for a, b in taps:
        term = None
        for f in range(frames):
            part = jnp.dot(inputs[f], window(f, a, b), preferred_element_type=jnp.float32)
            term = part if term is None else term + part
        for c in range(3):
            block = term[:, c * channels : (c + 1) * channels]
            kg_ref[(a * 3 + b) * 3 + c] = block.astype(kg_ref.dtype)
    for f in range(frames):
        total = None
        for a, b in taps:
            part = jnp.dot(window(f, a, b), k_ref[a * 3 + b], preferred_element_type=jnp.float32)
            total = part if total is None else total + part
        if not last:
            total = total * silu_slope(pre_ref[f].reshape(rows * cols, channels))
        out_ref[f] = total.astype(out_ref.dtype).reshape(rows, cols, channels)


def layer(wide, saved, pre, flipped, last):
    frames, rows, cols, channels = saved.shape
    return pl.pallas_call(
        functools.partial(convolve, last, not last),
        out_shape=(
            jax.ShapeDtypeStruct((27, channels, channels), jnp.bfloat16),
            jax.ShapeDtypeStruct(saved.shape, jnp.bfloat16),
        ),
        in_specs=[VMEM] * 4,
        out_specs=(VMEM, VMEM),
        scratch_shapes=[pltpu.VMEM((frames + 2, rows + 2, cols, 3 * channels), jnp.bfloat16)],
        compiler_params=pltpu.CompilerParams(vmem_limit_bytes=40 * 1024 * 1024),
        cost_estimate=pl.CostEstimate(
            flops=4 * 27 * frames * rows * cols * channels * channels,
            bytes_accessed=5_000_000,
            transcendentals=0,
        ),
        name="layer",
    )(wide, saved, pre, flipped)


def shards(
    layer_input, pre_one, pre_two, pre_three, kernel_one, kernel_two, kernel_three, upstream
):
    frame_count, row_count, col_count, channels = layer_input.shape
    ta_n, ha_n = lax.axis_size("ta"), lax.axis_size("ha")
    cells_total = frame_count * row_count * col_count * ta_n * ha_n
    norm_scale = 1.0 / math.sqrt(cells_total)
    gradient = (upstream.astype(jnp.float32) * silu_slope(pre_three)).astype(jnp.bfloat16)
    layers = [
        (kernel_three, pre_two, False),
        (kernel_two, pre_one, False),
        (kernel_one, layer_input, True),
    ]
    reduced = []
    for kernel, saved, last in layers:
        flipped = jnp.swapaxes(kernel, 3, 4).reshape(9, 3 * channels, channels)
        term, gradient = layer(halo(gradient, ta_n, ha_n), saved, saved, flipped, last)
        term = term.reshape(3, 3, 3, channels, channels)
        piece = lax.psum_scatter(term, "ha", scatter_dimension=3, tiled=True)
        total = lax.psum(piece.astype(jnp.float32), "ta")
        reduced.append(total * norm_scale)
    return (gradient, reduced[2], reduced[1], reduced[0])


def solution(mesh):
    return jax.shard_map(
        shards,
        mesh=mesh,
        in_specs=(
            P("ta", "ha", None, None),
            P("ta", "ha", None, None),
            P("ta", "ha", None, None),
            P("ta", "ha", None, None),
            P(),
            P(),
            P(),
            P("ta", "ha", None, None),
        ),
        out_specs=(
            P("ta", "ha", None, None),
            P(None, None, None, "ha", None),
            P(None, None, None, "ha", None),
            P(None, None, None, "ha", None),
        ),
        check_vma=False,
    )
```

```python
import functools
import math

import jax
import jax.numpy as jnp
from jax import lax
from jax.experimental import pallas as pl
from jax.experimental.pallas import tpu as pltpu
from jax.sharding import PartitionSpec as P

MESH = pl.DeviceIdType.MESH
VMEM = pl.BlockSpec(memory_space=pltpu.VMEM)


def silu_slope(pre_values):
    values = pre_values.astype(jnp.float32)
    sigmoid = jax.nn.sigmoid(values)
    return sigmoid * (1.0 + values * (1.0 - sigmoid))


def exchange(ta_n, ha_n, g_ref, out_ref, send_sems, recv_sems):
    ta, ha = lax.axis_index("ta"), lax.axis_index("ha")
    frames, rows = g_ref.shape[0], g_ref.shape[1]
    has_up, has_down = ha > 0, ha < ha_n - 1
    has_earlier, has_later = ta > 0, ta < ta_n - 1
    barrier = pltpu.get_barrier_semaphore()

    def device(d_ta, d_ha):
        return (ha + d_ha, ta + d_ta)

    def copy(index, source, target, d_ta, d_ha):
        return pltpu.make_async_remote_copy(
            src_ref=source,
            dst_ref=target,
            send_sem=send_sems.at[index],
            recv_sem=recv_sems.at[index],
            device_id=device(d_ta, d_ha),
            device_id_type=MESH,
        )

    for there, d_ta, d_ha in ((has_up, 0, -1), (has_down, 0, 1), (has_later, 1, 0)):

        @pl.when(there)
        def _():
            pl.semaphore_signal(barrier, inc=1, device_id=device(d_ta, d_ha), device_id_type=MESH)

    below = copy(0, g_ref.at[:, rows - 1], out_ref.at[pl.ds(0, frames), 0], 0, 1)
    above = copy(1, g_ref.at[:, 0], out_ref.at[pl.ds(0, frames), rows + 1], 0, -1)
    earlier = copy(2, g_ref, out_ref.at[pl.ds(frames, 2), pl.ds(1, rows)], -1, 0)
    corner_top = copy(3, out_ref.at[pl.ds(0, frames), 0], out_ref.at[pl.ds(frames, 2), 0], -1, 0)
    corner_end = copy(
        4, out_ref.at[pl.ds(0, frames), rows + 1], out_ref.at[pl.ds(frames, 2), rows + 1], -1, 0
    )
    peers = has_up.astype(jnp.int32) + has_down.astype(jnp.int32) + has_earlier.astype(jnp.int32)
    pl.semaphore_wait(barrier, peers)
    pl.when(has_down)(below.start)
    pl.when(has_up)(above.start)
    pl.when(has_earlier)(earlier.start)
    zero_row = jnp.zeros((frames,) + g_ref.shape[2:], g_ref.dtype)

    @pl.when(jnp.logical_not(has_up))
    def _():
        out_ref[0:frames, 0] = zero_row
        out_ref[frames : frames + 2, 0] = zero_row

    @pl.when(jnp.logical_not(has_down))
    def _():
        out_ref[0:frames, rows + 1] = zero_row
        out_ref[frames : frames + 2, rows + 1] = zero_row

    @pl.when(jnp.logical_not(has_later))
    def _():
        for row in range(rows + 2):
            out_ref[frames : frames + 2, row] = zero_row

    out_ref[0:frames, 1 : rows + 1] = g_ref[...]

    @pl.when(has_up)
    def _():
        below.wait_recv()

        @pl.when(has_earlier)
        def _():
            corner_top.start()

    @pl.when(has_down)
    def _():
        above.wait_recv()

        @pl.when(has_earlier)
        def _():
            corner_end.start()

    @pl.when(has_later)
    def _():
        earlier.wait_recv()
        pl.when(has_up)(corner_top.wait_recv)
        pl.when(has_down)(corner_end.wait_recv)

    pl.when(has_down)(below.wait_send)
    pl.when(has_up)(above.wait_send)

    @pl.when(has_earlier)
    def _():
        earlier.wait_send()
        pl.when(has_up)(corner_top.wait_send)
        pl.when(has_down)(corner_end.wait_send)


def halo(gradient, ta_n, ha_n):
    frames, rows, cols, channels = gradient.shape
    return pl.pallas_call(
        functools.partial(exchange, ta_n, ha_n),
        out_shape=jax.ShapeDtypeStruct((frames + 2, rows + 2, cols, channels), gradient.dtype),
        in_specs=[VMEM],
        out_specs=VMEM,
        scratch_shapes=[pltpu.SemaphoreType.DMA((5,)), pltpu.SemaphoreType.DMA((5,))],
        compiler_params=pltpu.CompilerParams(collective_id=0, has_side_effects=True),
        name="halo",
    )(gradient)


def convolve(last, act, wide_ref, x_ref, pre_ref, k_ref, kg_ref, out_ref, shifted):
    frames, rows, cols, channels = x_ref.shape
    column = lax.broadcasted_iota(jnp.int32, (cols, channels), 0)
    for f in range(frames + 2):
        for r in range(rows + 2):
            line = wide_ref[f, r]
            wide = line.astype(jnp.float32)
            after = jnp.where(column < cols - 1, pltpu.roll(wide, cols - 1, 0), 0.0)
            before = jnp.where(column > 0, pltpu.roll(wide, 1, 0), 0.0)
            shifted[f, r, :, 0:channels] = after.astype(line.dtype)
            shifted[f, r, :, channels : 2 * channels] = line
            shifted[f, r, :, 2 * channels : 3 * channels] = before.astype(line.dtype)

    def window(f, a, b):
        return shifted[f + 2 - a, 2 - b : 2 - b + rows].reshape(rows * cols, 3 * channels)

    taps = [(a, b) for a in range(3) for b in range(3)]
    pieces = kg_ref.shape[:2] + kg_ref.shape[5:]
    kg_ref[:, :, 1, 1, 6] = jnp.zeros(pieces, kg_ref.dtype)
    inputs = []
    for f in range(frames):
        values = x_ref[f].reshape(rows * cols, channels)
        if act:
            wide = values.astype(jnp.float32)
            values = (wide * jax.nn.sigmoid(wide)).astype(jnp.bfloat16)
        inputs.append(values.T)
    for a, b in taps:
        term = None
        for f in range(frames):
            part = jnp.dot(inputs[f], window(f, a, b), preferred_element_type=jnp.float32)
            term = part if term is None else term + part
        for c in range(3):
            block = term[:, c * channels : (c + 1) * channels].astype(kg_ref.dtype)
            tap = (a * 3 + b) * 3 + c
            kg_ref[:, :, tap // 14, tap // 7 % 2, tap % 7] = block.reshape(pieces)
    for f in range(frames):
        total = None
        for a, b in taps:
            part = jnp.dot(window(f, a, b), k_ref[a * 3 + b], preferred_element_type=jnp.float32)
            total = part if total is None else total + part
        if not last:
            total = total * silu_slope(pre_ref[f].reshape(rows * cols, channels))
        out_ref[f] = total.astype(out_ref.dtype).reshape(rows, cols, channels)


def layer(wide, saved, pre, flipped, last, ha_n):
    frames, rows, cols, channels = saved.shape
    return pl.pallas_call(
        functools.partial(convolve, last, not last),
        out_shape=(
            jax.ShapeDtypeStruct(
                (ha_n // 2, 2, 2, 2, 7, channels // ha_n, channels), jnp.bfloat16
            ),
            jax.ShapeDtypeStruct(saved.shape, jnp.bfloat16),
        ),
        in_specs=[VMEM] * 4,
        out_specs=(VMEM, VMEM),
        scratch_shapes=[pltpu.VMEM((frames + 2, rows + 2, cols, 3 * channels), jnp.bfloat16)],
        compiler_params=pltpu.CompilerParams(vmem_limit_bytes=40 * 1024 * 1024),
        cost_estimate=pl.CostEstimate(
            flops=4 * 27 * frames * rows * cols * channels * channels,
            bytes_accessed=5_000_000,
            transcendentals=0,
        ),
        name="layer",
    )(wide, saved, pre, flipped)


def added(one, two):
    return (one.astype(jnp.float32) + two.astype(jnp.float32)).astype(jnp.bfloat16)


def reduce_shapes(term_shape):
    depth, tail = term_shape[0], term_shape[4:]
    half = depth // 2
    shapes = [
        (depth, 2, 2) + tail,
        (depth, 2, 2) + tail,
        (half, 2) + tail,
        (half, 2) + tail,
        (half,) + tail,
        (half, 2) + tail,
        (half, 2) + tail,
        (half,) + tail,
        (depth,) + tail,
        (depth - 1,) + tail,
        (4,) + tail,
    ]
    return [pltpu.VMEM(shape, jnp.bfloat16) for shape in shapes]


def reduce_sems(depth):
    return 5 + depth - 1 + 3


def reduce_peers(depth):
    ta, ha = lax.axis_index("ta"), lax.axis_index("ha")
    z, x, y, core = ha // 2, ha % 2, ta // 2, ta % 2
    across_core = (ha, y * 2 + 1 - core)
    across_y = (ha, (1 - y) * 2 + core)
    across_x = (z * 2 + 1 - x, ta)
    along_z = [((z + step) % depth * 2 + x, ta) for step in range(1, depth)]
    around = [(ha, (ta + step) % 4) for step in range(1, 4)]
    return across_core, across_y, across_x, along_z, around


def reduce_phases(term, out_ref, buffers, send_sems, recv_sems, scale):
    depth = term.shape[0]
    half = depth // 2
    ta, ha = lax.axis_index("ta"), lax.axis_index("ha")
    z, x, y, core = ha // 2, ha % 2, ta // 2, ta % 2
    across_core, across_y, across_x, along_z, around = reduce_peers(depth)
    from_core, cores, low_x, low, low_y, top_y, top, top_x, rest, from_z, whole = buffers

    def copy(index, source, target, peer):
        return pltpu.make_async_remote_copy(
            src_ref=source,
            dst_ref=target,
            send_sem=send_sems.at[index],
            recv_sem=recv_sems.at[index],
            device_id=peer,
            device_id_type=MESH,
        )

    core_copy = copy(0, term.at[:, :, :, 1 - core], from_core, across_core)
    low_x_copy = copy(1, cores.at[pl.ds(0, half), 1 - x], low_x, across_x)
    low_y_copy = copy(2, low.at[:, 1 - y], low_y, across_y)
    top_y_copy = copy(3, cores.at[pl.ds(half, half), :, 1 - y], top_y, across_y)
    top_x_copy = copy(4, top.at[:, 1 - x], top_x, across_x)
    z_copies = [
        copy(5 + step, rest.at[(z + step + 1) % depth], from_z.at[step], along_z[step])
        for step in range(depth - 1)
    ]
    last_copies = [
        copy(4 + depth + step, whole.at[ta], whole.at[ta], around[step]) for step in range(3)
    ]

    def start():
        core_copy.start()

    def first():
        core_copy.wait_recv()
        for row in range(half):
            cores[row] = added(term[row, :, :, core], from_core[row])
        low_x_copy.start()
        for row in range(half, depth):
            cores[row] = added(term[row, :, :, core], from_core[row])
        top_y_copy.start()

    def second():
        low_x_copy.wait_recv()
        low[...] = added(cores[0:half, x], low_x[...])
        low_y_copy.start()
        top_y_copy.wait_recv()
        top[...] = added(cores[half:depth, :, y], top_y[...])
        top_x_copy.start()

    def third():
        low_y_copy.wait_recv()
        rest[0:half] = added(low[:, y], low_y[...])
        top_x_copy.wait_recv()
        rest[half:depth] = added(top[:, x], top_x[...])
        for each in z_copies:
            each.start()

    def fourth():
        total = rest[z].astype(jnp.float32)
        for step in range(depth - 1):
            z_copies[step].wait_recv()
            total = total + from_z[step].astype(jnp.float32)
        whole[ta] = total.astype(jnp.bfloat16)
        for each in last_copies:
            each.start()

    def finish():
        for each in last_copies:
            each.wait_recv()
        for tap in range(27):
            out_ref[tap] = whole[tap // 7, tap % 7].astype(jnp.float32) * scale
        for each in [core_copy, low_x_copy, low_y_copy, top_y_copy, top_x_copy] + z_copies + last_copies:
            each.wait_send()

    return [start, first, second, third, fourth, finish]


def greet_reducers(depth):
    barrier = pltpu.get_barrier_semaphore()
    _, _, across_x, along_z, around = reduce_peers(depth)
    peers = [across_x] + along_z + around
    for peer in peers:
        pl.semaphore_signal(barrier, inc=1, device_id=peer, device_id_type=MESH)
    pl.semaphore_wait(barrier, len(peers))


def reducer(scale, count, *refs):
    terms, outs = refs[:count], refs[count : 2 * count]
    buffers = refs[2 * count : -2]
    send_sems, recv_sems = refs[-2:]
    greet_reducers(terms[0].shape[0])
    each = len(buffers) // count
    stages = [
        reduce_phases(
            terms[n],
            outs[n],
            buffers[n * each : (n + 1) * each],
            send_sems.at[n],
            recv_sems.at[n],
            scale,
        )
        for n in range(count)
    ]
    for turn in range(len(stages[0]) + count - 1):
        for n in range(count):
            if 0 <= turn - n < len(stages[0]):
                stages[n][turn - n]()


def reduce_terms(terms, scale):
    count, shape = len(terms), terms[0].shape
    sems = reduce_sems(shape[0])
    return pl.pallas_call(
        functools.partial(reducer, scale, count),
        out_shape=[jax.ShapeDtypeStruct((27,) + shape[5:], jnp.float32)] * count,
        in_specs=[VMEM] * count,
        out_specs=[VMEM] * count,
        scratch_shapes=reduce_shapes(shape) * count
        + [pltpu.SemaphoreType.DMA((count, sems)), pltpu.SemaphoreType.DMA((count, sems))],
        compiler_params=pltpu.CompilerParams(
            collective_id=1, has_side_effects=True, vmem_limit_bytes=48 * 1024 * 1024
        ),
        name="reduce",
    )(*terms)


def shards(
    layer_input, pre_one, pre_two, pre_three, kernel_one, kernel_two, kernel_three, upstream
):
    frame_count, row_count, col_count, channels = layer_input.shape
    ta_n, ha_n = lax.axis_size("ta"), lax.axis_size("ha")
    cells_total = frame_count * row_count * col_count * ta_n * ha_n
    norm_scale = 1.0 / math.sqrt(cells_total)
    gradient = (upstream.astype(jnp.float32) * silu_slope(pre_three)).astype(jnp.bfloat16)
    layers = [
        (kernel_three, pre_two, False),
        (kernel_two, pre_one, False),
        (kernel_one, layer_input, True),
    ]
    terms = []
    for kernel, saved, last in layers:
        flipped = jnp.swapaxes(kernel, 3, 4).reshape(9, 3 * channels, channels)
        term, gradient = layer(halo(gradient, ta_n, ha_n), saved, saved, flipped, last, ha_n)
        terms.append(term)
    reduced = reduce_terms(terms, norm_scale)
    reduced = [total.reshape(3, 3, 3, channels // ha_n, channels) for total in reduced]
    return (gradient, reduced[2], reduced[1], reduced[0])


def solution(mesh):
    return jax.shard_map(
        shards,
        mesh=mesh,
        in_specs=(
            P("ta", "ha", None, None),
            P("ta", "ha", None, None),
            P("ta", "ha", None, None),
            P("ta", "ha", None, None),
            P(),
            P(),
            P(),
            P("ta", "ha", None, None),
        ),
        out_specs=(
            P("ta", "ha", None, None),
            P(None, None, None, "ha", None),
            P(None, None, None, "ha", None),
            P(None, None, None, "ha", None),
        ),
        check_vma=False,
    )
```

```python
import functools
import math

import jax
import jax.numpy as jnp
from jax import lax
from jax.experimental import pallas as pl
from jax.experimental.pallas import tpu as pltpu
from jax.sharding import PartitionSpec as P

MESH = pl.DeviceIdType.MESH
VMEM = pl.BlockSpec(memory_space=pltpu.VMEM)


def silu_slope(pre_values):
    values = pre_values.astype(jnp.float32)
    sigmoid = jax.nn.sigmoid(values)
    return sigmoid * (1.0 + values * (1.0 - sigmoid))


def halo_stages(ta_n, ha_n, wide, send_sems, recv_sems):
    ta, ha = lax.axis_index("ta"), lax.axis_index("ha")
    frames, rows = wide.shape[0] - 2, wide.shape[1] - 2
    has_up, has_down = ha > 0, ha < ha_n - 1
    has_earlier, has_later = ta > 0, ta < ta_n - 1

    def copy(index, source, target, d_ta, d_ha):
        return pltpu.make_async_remote_copy(
            src_ref=source,
            dst_ref=target,
            send_sem=send_sems.at[index],
            recv_sem=recv_sems.at[index],
            device_id=(ha + d_ha, ta + d_ta),
            device_id_type=MESH,
        )

    now, ahead = pl.ds(0, frames), pl.ds(frames, 2)
    below = copy(0, wide.at[now, rows], wide.at[now, 0], 0, 1)
    above = copy(1, wide.at[now, 1], wide.at[now, rows + 1], 0, -1)
    earlier = copy(2, wide.at[now, pl.ds(1, rows)], wide.at[ahead, pl.ds(1, rows)], -1, 0)
    corner_top = copy(3, wide.at[now, 0], wide.at[ahead, 0], -1, 0)
    corner_end = copy(4, wide.at[now, rows + 1], wide.at[ahead, rows + 1], -1, 0)

    def clear():
        zero_row = jnp.zeros((frames,) + wide.shape[2:], wide.dtype)

        @pl.when(jnp.logical_not(has_up))
        def _():
            wide[0:frames, 0] = zero_row
            wide[frames : frames + 2, 0] = zero_row

        @pl.when(jnp.logical_not(has_down))
        def _():
            wide[0:frames, rows + 1] = zero_row
            wide[frames : frames + 2, rows + 1] = zero_row

        @pl.when(jnp.logical_not(has_later))
        def _():
            for row in range(rows + 2):
                wide[frames : frames + 2, row] = zero_row

    def start():
        pl.when(has_down)(below.start)
        pl.when(has_up)(above.start)
        pl.when(has_earlier)(earlier.start)

    def corners():
        @pl.when(has_up)
        def _():
            below.wait_recv()
            pl.when(has_earlier)(corner_top.start)

        @pl.when(has_down)
        def _():
            above.wait_recv()
            pl.when(has_earlier)(corner_end.start)

    def arrive():
        @pl.when(has_later)
        def _():
            earlier.wait_recv()
            pl.when(has_up)(corner_top.wait_recv)
            pl.when(has_down)(corner_end.wait_recv)

    def finish():
        pl.when(has_down)(below.wait_send)
        pl.when(has_up)(above.wait_send)

        @pl.when(has_earlier)
        def _():
            earlier.wait_send()
            pl.when(has_up)(corner_top.wait_send)
            pl.when(has_down)(corner_end.wait_send)

    return clear, start, corners, arrive, finish


def shift(wide, shifted, f, first, count):
    cols, channels = wide.shape[2:]
    size = count * cols
    column = lax.broadcasted_iota(jnp.int32, (count, cols, channels), 1).reshape(size, channels)
    lines = wide[f, first : first + count]
    flat = lines.reshape(size, channels).astype(jnp.float32)
    after = jnp.where(column < cols - 1, pltpu.roll(flat, size - 1, 0), 0.0)
    before = jnp.where(column > 0, pltpu.roll(flat, 1, 0), 0.0)
    for place, values in ((0, after.astype(lines.dtype)), (2, before.astype(lines.dtype))):
        shifted[f, first : first + count, :, place * channels : (place + 1) * channels] = (
            values.reshape(lines.shape)
        )
    shifted[f, first : first + count, :, channels : 2 * channels] = lines


TAPS = [(a, b) for a in range(3) for b in range(3)]


def window(shifted, f, a, b):
    rows, cols, width = shifted.shape[1] - 2, shifted.shape[2], shifted.shape[3]
    return shifted[f + 2 - a, 2 - b : 2 - b + rows].reshape(rows * cols, width)


def kernel_term(turned, shifted, term):
    channels = turned.shape[1]
    pieces = term.shape[:2] + term.shape[5:]
    term[:, :, 1, 1, 6] = jnp.zeros(pieces, term.dtype)
    for a, b in TAPS:
        total = None
        for f in range(turned.shape[0]):
            part = jnp.dot(turned[f], window(shifted, f, a, b), preferred_element_type=jnp.float32)
            total = part if total is None else total + part
        for c in range(3):
            block = total[:, c * channels : (c + 1) * channels].astype(term.dtype)
            tap = (a * 3 + b) * 3 + c
            term[:, :, tap // 14, tap // 7 % 2, tap % 7] = block.reshape(pieces)


def back(shifted, flipped, f):
    total = None
    for a, b in TAPS:
        part = jnp.dot(
            window(shifted, f, a, b), flipped[a * 3 + b], preferred_element_type=jnp.float32
        )
        total = part if total is None else total + part
    return total


def added(one, two):
    return (one.astype(jnp.float32) + two.astype(jnp.float32)).astype(jnp.bfloat16)


def reduce_shapes(term_shape):
    depth, tail = term_shape[0], term_shape[4:]
    half = depth // 2
    shapes = [
        (depth, 2, 2) + tail,
        (depth, 2, 2) + tail,
        (half, 2) + tail,
        (half, 2) + tail,
        (half,) + tail,
        (half, 2) + tail,
        (half, 2) + tail,
        (half,) + tail,
        (depth,) + tail,
        (depth - 1,) + tail,
        (4,) + tail,
    ]
    return [pltpu.VMEM(shape, jnp.bfloat16) for shape in shapes]


def reduce_sems(depth):
    return 5 + depth - 1 + 3


def reduce_peers(depth):
    ta, ha = lax.axis_index("ta"), lax.axis_index("ha")
    z, x, y, core = ha // 2, ha % 2, ta // 2, ta % 2
    across_core = (ha, y * 2 + 1 - core)
    across_y = (ha, (1 - y) * 2 + core)
    across_x = (z * 2 + 1 - x, ta)
    along_z = [((z + step) % depth * 2 + x, ta) for step in range(1, depth)]
    around = [(ha, (ta + step) % 4) for step in range(1, 4)]
    return across_core, across_y, across_x, along_z, around


def reduce_phases(term, out_ref, buffers, send_sems, recv_sems, scale):
    depth = term.shape[0]
    half = depth // 2
    ta, ha = lax.axis_index("ta"), lax.axis_index("ha")
    z, x, y, core = ha // 2, ha % 2, ta // 2, ta % 2
    across_core, across_y, across_x, along_z, around = reduce_peers(depth)
    from_core, cores, low_x, low, low_y, top_y, top, top_x, rest, from_z, whole = buffers

    def copy(index, source, target, peer):
        return pltpu.make_async_remote_copy(
            src_ref=source,
            dst_ref=target,
            send_sem=send_sems.at[index],
            recv_sem=recv_sems.at[index],
            device_id=peer,
            device_id_type=MESH,
        )

    core_copy = copy(0, term.at[:, :, :, 1 - core], from_core, across_core)
    low_x_copy = copy(1, cores.at[pl.ds(0, half), 1 - x], low_x, across_x)
    low_y_copy = copy(2, low.at[:, 1 - y], low_y, across_y)
    top_y_copy = copy(3, cores.at[pl.ds(half, half), :, 1 - y], top_y, across_y)
    top_x_copy = copy(4, top.at[:, 1 - x], top_x, across_x)
    z_copies = [
        copy(5 + step, rest.at[(z + step + 1) % depth], from_z.at[step], along_z[step])
        for step in range(depth - 1)
    ]
    last_copies = [
        copy(4 + depth + step, whole.at[ta], whole.at[ta], around[step]) for step in range(3)
    ]

    def start():
        core_copy.start()

    def first():
        core_copy.wait_recv()
        for row in range(half):
            cores[row] = added(term[row, :, :, core], from_core[row])
        low_x_copy.start()
        for row in range(half, depth):
            cores[row] = added(term[row, :, :, core], from_core[row])
        top_y_copy.start()

    def second():
        low_x_copy.wait_recv()
        low[...] = added(cores[0:half, x], low_x[...])
        low_y_copy.start()
        top_y_copy.wait_recv()
        top[...] = added(cores[half:depth, :, y], top_y[...])
        top_x_copy.start()

    def third():
        low_y_copy.wait_recv()
        rest[0:half] = added(low[:, y], low_y[...])
        top_x_copy.wait_recv()
        rest[half:depth] = added(top[:, x], top_x[...])
        for each in z_copies:
            each.start()

    def fourth():
        total = rest[z].astype(jnp.float32)
        for step in range(depth - 1):
            z_copies[step].wait_recv()
            total = total + from_z[step].astype(jnp.float32)
        whole[ta] = total.astype(jnp.bfloat16)
        for each in last_copies:
            each.start()

    def finish():
        for each in last_copies:
            each.wait_recv()
        for tap in range(27):
            out_ref[tap] = whole[tap // 7, tap % 7].astype(jnp.float32) * scale
        for each in [core_copy, low_x_copy, low_y_copy, top_y_copy, top_x_copy] + z_copies + last_copies:
            each.wait_send()

    return [start, first, second, third, fourth, finish]


def greet(ha_n):
    barrier = pltpu.get_barrier_semaphore()
    ta, ha = lax.axis_index("ta"), lax.axis_index("ha")
    _, _, across_x, along_z, around = reduce_peers(ha_n // 2)
    peers = [across_x] + along_z + around
    for peer in peers:
        pl.semaphore_signal(barrier, inc=1, device_id=peer, device_id_type=MESH)
    other = ha - 1 + ha % 2 * 2
    exists = jnp.logical_and(other >= 0, other < ha_n)

    @pl.when(exists)
    def _():
        pl.semaphore_signal(barrier, inc=1, device_id=(other, ta), device_id_type=MESH)

    pl.semaphore_wait(barrier, len(peers) + exists.astype(jnp.int32))


def whole_kernel(ta_n, ha_n, scale, *refs):
    upstream, pre_three, saved_hbm, kernels_hbm = refs[0], refs[1], refs[2:5], refs[5:8]
    input_gradient, outs = refs[8], refs[9:12]
    saved, kernels, wides, terms = refs[12:15], refs[15:18], refs[18:21], refs[21:24]
    shifted, flipped, turned, slopes = refs[24:28]
    load_sems, halo_send, halo_recv, send_sems, recv_sems = refs[-5:]
    buffers = refs[28:-5]
    each = len(buffers) // 3
    frames, rows, cols, channels = upstream.shape
    size = rows * cols

    loads = [
        pltpu.make_async_copy(source, target, load_sems.at[n])
        for n, (source, target) in enumerate(
            zip(tuple(saved_hbm) + tuple(kernels_hbm), tuple(saved) + tuple(kernels))
        )
    ]
    for n in (0, 3, 1, 4, 2, 5):
        loads[n].start()
    halos = [
        halo_stages(ta_n, ha_n, wides[n], halo_send.at[n], halo_recv.at[n]) for n in range(3)
    ]
    sums = [
        reduce_phases(
            terms[n], outs[n], buffers[n * each : (n + 1) * each], send_sems.at[n], recv_sems.at[n], scale
        )
        for n in range(3)
    ]
    for f in range(frames):
        values = upstream[f].astype(jnp.float32) * silu_slope(pre_three[f])
        wides[0][f, 1 : rows + 1] = values.astype(jnp.bfloat16)
    greet(ha_n)
    halos[0][1]()
    for clear, _, _, _, _ in halos:
        clear()

    for n in range(3):
        _, _, corners, arrive, _ = halos[n]
        if n > 0:
            kernel_term(turned, shifted, terms[n - 1])
            sums[n - 1][0]()
        if n > 1:
            sums[n - 2][2]()
        loads[n].wait()
        loads[3 + n].wait()
        for f in range(frames):
            values = saved[n][f].reshape(size, channels)
            if n < 2:
                slopes[f] = silu_slope(values)
                wide = values.astype(jnp.float32)
                values = (wide * jax.nn.sigmoid(wide)).astype(jnp.bfloat16)
            turned[f] = values.T
        for a, b in TAPS:
            for c in range(3):
                flipped[a * 3 + b, c * channels : (c + 1) * channels] = kernels[n][a, b, c].T
        for f in range(frames):
            shift(wides[n], shifted, f, 1, rows)
        corners()
        for f in range(frames):
            shift(wides[n], shifted, f, 0, 1)
            shift(wides[n], shifted, f, rows + 1, 1)
        if n > 1:
            sums[n - 2][3]()
        arrive()
        if n > 0:
            sums[n - 1][1]()
        for f in range(frames, frames + 2):
            shift(wides[n], shifted, f, 0, rows + 2)
        if n == 2:
            kernel_term(turned, shifted, terms[n])
            sums[n][0]()
        for f in range(frames):
            total = back(shifted, flipped, f)
            if n < 2:
                total = total * slopes[f]
                wides[n + 1][f, 1 : rows + 1] = total.astype(jnp.bfloat16).reshape(
                    rows, cols, channels
                )
            else:
                input_gradient[f] = total.astype(jnp.bfloat16).reshape(rows, cols, channels)
                if f == 0:
                    sums[n][1]()
                    sums[n - 1][2]()
        if n < 2:
            halos[n + 1][1]()
    sums[0][4]()
    sums[2][2]()
    sums[1][3]()
    sums[2][3]()
    sums[1][4]()
    sums[2][4]()
    sums[0][5]()
    sums[1][5]()
    sums[2][5]()
    for halo in halos:
        halo[4]()


def shards(
    layer_input, pre_one, pre_two, pre_three, kernel_one, kernel_two, kernel_three, upstream
):
    frames, rows, cols, channels = layer_input.shape
    ta_n, ha_n = lax.axis_size("ta"), lax.axis_size("ha")
    scale = 1.0 / math.sqrt(frames * rows * cols * ta_n * ha_n)
    piece = channels // ha_n
    term_shape = (ha_n // 2, 2, 2, 2, 7, piece, channels)
    sems = reduce_sems(ha_n // 2)
    anywhere = pl.BlockSpec(memory_space=pl.ANY)
    half = jnp.bfloat16
    scratch = (
        [pltpu.VMEM(layer_input.shape, half)] * 3
        + [pltpu.VMEM(kernel_one.shape, half)] * 3
        + [pltpu.VMEM((frames + 2, rows + 2, cols, channels), half)] * 3
        + [pltpu.VMEM(term_shape, half)] * 3
        + [
            pltpu.VMEM((frames + 2, rows + 2, cols, 3 * channels), half),
            pltpu.VMEM((9, 3 * channels, channels), half),
            pltpu.VMEM((frames, channels, rows * cols), half),
            pltpu.VMEM((frames, rows * cols, channels), jnp.float32),
        ]
        + reduce_shapes(term_shape) * 3
        + [
            pltpu.SemaphoreType.DMA((6,)),
            pltpu.SemaphoreType.DMA((3, 5)),
            pltpu.SemaphoreType.DMA((3, 5)),
            pltpu.SemaphoreType.DMA((3, sems)),
            pltpu.SemaphoreType.DMA((3, sems)),
        ]
    )
    result = pl.pallas_call(
        functools.partial(whole_kernel, ta_n, ha_n, scale),
        out_shape=[jax.ShapeDtypeStruct(layer_input.shape, half)]
        + [jax.ShapeDtypeStruct((27, piece, channels), jnp.float32)] * 3,
        in_specs=[VMEM] * 2 + [anywhere] * 6,
        out_specs=[VMEM] * 4,
        scratch_shapes=scratch,
        compiler_params=pltpu.CompilerParams(
            collective_id=0, has_side_effects=True, vmem_limit_bytes=56 * 1024 * 1024
        ),
        name="backward",
    )(upstream, pre_three, pre_two, pre_one, layer_input, kernel_three, kernel_two, kernel_one)
    input_gradient, *sums = result
    three, two, one = [total.reshape(3, 3, 3, piece, channels) for total in sums]
    return (input_gradient, one, two, three)


def solution(mesh):
    return jax.shard_map(
        shards,
        mesh=mesh,
        in_specs=(
            P("ta", "ha", None, None),
            P("ta", "ha", None, None),
            P("ta", "ha", None, None),
            P("ta", "ha", None, None),
            P(),
            P(),
            P(),
            P("ta", "ha", None, None),
        ),
        out_specs=(
            P("ta", "ha", None, None),
            P(None, None, None, "ha", None),
            P(None, None, None, "ha", None),
            P(None, None, None, "ha", None),
        ),
        check_vma=False,
    )
```

```python
import functools
import math

import jax
import jax.numpy as jnp
from jax import lax
from jax.experimental import pallas as pl
from jax.experimental.pallas import tpu as pltpu
from jax.sharding import PartitionSpec as P

MESH = pl.DeviceIdType.MESH
VMEM = pl.BlockSpec(memory_space=pltpu.VMEM)


def silu_slope(pre_values):
    values = pre_values.astype(jnp.float32)
    sigmoid = jax.nn.sigmoid(values)
    return sigmoid * (1.0 + values * (1.0 - sigmoid))


def halo_stages(ta_n, ha_n, wide, send_sems, recv_sems):
    ta, ha = lax.axis_index("ta"), lax.axis_index("ha")
    frames, rows = wide.shape[0] - 2, wide.shape[1] - 2
    has_up, has_down = ha > 0, ha < ha_n - 1
    has_earlier, has_later = ta > 0, ta < ta_n - 1

    def copy(index, source, target, d_ta, d_ha):
        return pltpu.make_async_remote_copy(
            src_ref=source,
            dst_ref=target,
            send_sem=send_sems.at[index],
            recv_sem=recv_sems.at[index],
            device_id=(ha + d_ha, ta + d_ta),
            device_id_type=MESH,
        )

    now, ahead = pl.ds(0, frames), pl.ds(frames, 2)
    each = range(frames)
    below = [copy(1 + 4 * f, wide.at[f, rows], wide.at[f, 0], 0, 1) for f in each]
    above = [copy(2 + 4 * f, wide.at[f, 1], wide.at[f, rows + 1], 0, -1) for f in each]
    earlier = copy(0, wide.at[now, pl.ds(1, rows)], wide.at[ahead, pl.ds(1, rows)], -1, 0)
    corner_top = [copy(3 + 4 * f, wide.at[f, 0], wide.at[frames + f, 0], -1, 0) for f in each]
    corner_end = [
        copy(4 + 4 * f, wide.at[f, rows + 1], wide.at[frames + f, rows + 1], -1, 0) for f in each
    ]

    def clear():
        zero_row = jnp.zeros((frames,) + wide.shape[2:], wide.dtype)

        @pl.when(jnp.logical_not(has_up))
        def _():
            wide[0:frames, 0] = zero_row
            wide[frames : frames + 2, 0] = zero_row

        @pl.when(jnp.logical_not(has_down))
        def _():
            wide[0:frames, rows + 1] = zero_row
            wide[frames : frames + 2, rows + 1] = zero_row

        @pl.when(jnp.logical_not(has_later))
        def _():
            for row in range(rows + 2):
                wide[frames : frames + 2, row] = zero_row

    def start():
        for f in each:
            pl.when(has_down)(below[f].start)
            pl.when(has_up)(above[f].start)
        pl.when(has_earlier)(earlier.start)

    def corners():
        for f in each:

            @pl.when(has_up)
            def _():
                below[f].wait_recv()
                pl.when(has_earlier)(corner_top[f].start)

            @pl.when(has_down)
            def _():
                above[f].wait_recv()
                pl.when(has_earlier)(corner_end[f].start)

    def arrive_block():
        pl.when(has_later)(earlier.wait_recv)

    def arrive_corners():
        @pl.when(has_later)
        def _():
            for f in each:
                pl.when(has_up)(corner_top[f].wait_recv)
                pl.when(has_down)(corner_end[f].wait_recv)

    def finish():
        for f in each:
            pl.when(has_down)(below[f].wait_send)
            pl.when(has_up)(above[f].wait_send)

        @pl.when(has_earlier)
        def _():
            earlier.wait_send()
            for f in each:
                pl.when(has_up)(corner_top[f].wait_send)
                pl.when(has_down)(corner_end[f].wait_send)

    return clear, start, corners, arrive_block, arrive_corners, finish


def shift(wide, shifted, f, first, count):
    cols, channels = wide.shape[2:]
    size = count * cols
    column = lax.broadcasted_iota(jnp.int32, (count, cols, channels), 1).reshape(size, channels)
    lines = wide[f, first : first + count]
    flat = lines.reshape(size, channels).astype(jnp.float32)
    after = jnp.where(column < cols - 1, pltpu.roll(flat, size - 1, 0), 0.0)
    before = jnp.where(column > 0, pltpu.roll(flat, 1, 0), 0.0)
    for place, values in ((0, after.astype(lines.dtype)), (2, before.astype(lines.dtype))):
        shifted[f, first : first + count, :, place * channels : (place + 1) * channels] = (
            values.reshape(lines.shape)
        )
    shifted[f, first : first + count, :, channels : 2 * channels] = lines


TAPS = [(a, b) for a in range(3) for b in range(3)]


def window(shifted, f, a, b):
    rows, cols, width = shifted.shape[1] - 2, shifted.shape[2], shifted.shape[3]
    return shifted[f + 2 - a, 2 - b : 2 - b + rows].reshape(rows * cols, width)


def kernel_term(turned, shifted, term, steps=(0, 1, 2)):
    channels = turned.shape[1]
    pieces = term.shape[:2] + term.shape[5:]
    term[:, :, 1, 1, 6] = jnp.zeros(pieces, term.dtype)
    for a, b in TAPS:
        if a not in steps:
            continue
        total = None
        for f in range(turned.shape[0]):
            part = jnp.dot(turned[f], window(shifted, f, a, b), preferred_element_type=jnp.float32)
            total = part if total is None else total + part
        for c in range(3):
            block = total[:, c * channels : (c + 1) * channels].astype(term.dtype)
            tap = (a * 3 + b) * 3 + c
            term[:, :, tap // 14, tap // 7 % 2, tap % 7] = block.reshape(pieces)


def back(shifted, flipped, sums, ahead, side):
    frames = sums.shape[0]
    for f in range(frames):
        total = None
        for a, b in TAPS:
            if (f + 2 - a >= frames) != ahead or (b != 1) != side:
                continue
            part = jnp.dot(
                window(shifted, f, a, b), flipped[a * 3 + b], preferred_element_type=jnp.float32
            )
            total = part if total is None else total + part
        if ahead or side:
            total = sums[f] + total
        sums[f] = total


def added(one, two):
    return (one.astype(jnp.float32) + two.astype(jnp.float32)).astype(jnp.bfloat16)


def reduce_shapes(term_shape):
    depth, tail = term_shape[0], term_shape[4:]
    half = depth // 2
    shapes = [
        (depth, 2, 2) + tail,
        (depth, 2, 2) + tail,
        (half, 2) + tail,
        (half, 2) + tail,
        (half,) + tail,
        (half, 2) + tail,
        (half, 2) + tail,
        (half,) + tail,
        (depth,) + tail,
        (depth - 1,) + tail,
        (4,) + tail,
    ]
    return [pltpu.VMEM(shape, jnp.bfloat16) for shape in shapes]


def reduce_sems(depth):
    return 5 + depth - 1 + 3


def reduce_peers(depth):
    ta, ha = lax.axis_index("ta"), lax.axis_index("ha")
    z, x, y, core = ha // 2, ha % 2, ta // 2, ta % 2
    across_core = (ha, y * 2 + 1 - core)
    across_y = (ha, (1 - y) * 2 + core)
    across_x = (z * 2 + 1 - x, ta)
    along_z = [((z + step) % depth * 2 + x, ta) for step in range(1, depth)]
    around = [(ha, (ta + step) % 4) for step in range(1, 4)]
    return across_core, across_y, across_x, along_z, around


def reduce_phases(term, out_ref, buffers, send_sems, recv_sems, scale):
    depth = term.shape[0]
    half = depth // 2
    ta, ha = lax.axis_index("ta"), lax.axis_index("ha")
    z, x, y, core = ha // 2, ha % 2, ta // 2, ta % 2
    across_core, across_y, across_x, along_z, around = reduce_peers(depth)
    from_core, cores, low_x, low, low_y, top_y, top, top_x, rest, from_z, whole = buffers

    def copy(index, source, target, peer):
        return pltpu.make_async_remote_copy(
            src_ref=source,
            dst_ref=target,
            send_sem=send_sems.at[index],
            recv_sem=recv_sems.at[index],
            device_id=peer,
            device_id_type=MESH,
        )

    core_copy = copy(0, term.at[:, :, :, 1 - core], from_core, across_core)
    low_x_copy = copy(1, cores.at[pl.ds(0, half), 1 - x], low_x, across_x)
    low_y_copy = copy(2, low.at[:, 1 - y], low_y, across_y)
    top_y_copy = copy(3, cores.at[pl.ds(half, half), :, 1 - y], top_y, across_y)
    top_x_copy = copy(4, top.at[:, 1 - x], top_x, across_x)
    z_copies = [
        copy(5 + step, rest.at[(z + step + 1) % depth], from_z.at[step], along_z[step])
        for step in range(depth - 1)
    ]
    last_copies = [
        copy(4 + depth + step, whole.at[ta], whole.at[ta], around[step]) for step in range(3)
    ]

    def start():
        core_copy.start()

    def first():
        core_copy.wait_recv()
        for row in range(half):
            cores[row] = added(term[row, :, :, core], from_core[row])
        low_x_copy.start()

    def first_y():
        for row in range(half, depth):
            cores[row] = added(term[row, :, :, core], from_core[row])
        top_y_copy.start()

    def second():
        low_x_copy.wait_recv()
        low[...] = added(cores[0:half, x], low_x[...])
        low_y_copy.start()
        top_y_copy.wait_recv()
        top[...] = added(cores[half:depth, :, y], top_y[...])
        top_x_copy.start()

    def third():
        low_y_copy.wait_recv()
        rest[0:half] = added(low[:, y], low_y[...])
        top_x_copy.wait_recv()
        rest[half:depth] = added(top[:, x], top_x[...])
        for each in z_copies:
            each.start()

    def fourth():
        total = rest[z].astype(jnp.float32)
        for step in range(depth - 1):
            z_copies[step].wait_recv()
            total = total + from_z[step].astype(jnp.float32)
        whole[ta] = total.astype(jnp.bfloat16)
        for each in last_copies:
            each.start()

    def finish():
        for each in last_copies:
            each.wait_recv()
        for tap in range(27):
            out_ref[tap] = whole[tap // 7, tap % 7].astype(jnp.float32) * scale
        for each in [core_copy, low_x_copy, low_y_copy, top_y_copy, top_x_copy] + z_copies + last_copies:
            each.wait_send()

    return start, first, first_y, second, third, fourth, finish


def greet(ha_n):
    barrier = pltpu.get_barrier_semaphore()
    ta, ha = lax.axis_index("ta"), lax.axis_index("ha")
    _, _, across_x, along_z, around = reduce_peers(ha_n // 2)
    peers = [across_x] + along_z + around
    for peer in peers:
        pl.semaphore_signal(barrier, inc=1, device_id=peer, device_id_type=MESH)
    other = ha - 1 + ha % 2 * 2
    exists = jnp.logical_and(other >= 0, other < ha_n)

    @pl.when(exists)
    def _():
        pl.semaphore_signal(barrier, inc=1, device_id=(other, ta), device_id_type=MESH)

    return lambda: pl.semaphore_wait(barrier, len(peers) + exists.astype(jnp.int32))


def whole_kernel(ta_n, ha_n, scale, *refs):
    upstream, pre_three, saved_hbm, kernels_hbm = refs[0], refs[1], refs[2:5], refs[5:8]
    input_gradient, outs = refs[8], refs[9:12]
    saved, kernels, wides, terms = refs[12:15], refs[15:18], refs[18:21], refs[21:24]
    shifted, flipped, turned, slopes, totals = refs[24:29]
    load_sems, halo_send, halo_recv, send_sems, recv_sems = refs[-5:]
    buffers = refs[29:-5]
    each = len(buffers) // 3
    frames, rows, cols, channels = upstream.shape
    size = rows * cols
    gathered = greet(ha_n)

    loads = [
        pltpu.make_async_copy(source, target, load_sems.at[n])
        for n, (source, target) in enumerate(
            zip(tuple(saved_hbm) + tuple(kernels_hbm), tuple(saved) + tuple(kernels))
        )
    ]
    for n in (0, 3, 1, 4, 2, 5):
        loads[n].start()
    halos = [
        halo_stages(ta_n, ha_n, wides[n], halo_send.at[n], halo_recv.at[n]) for n in range(3)
    ]
    sums = [
        reduce_phases(
            terms[n], outs[n], buffers[n * each : (n + 1) * each], send_sems.at[n], recv_sems.at[n], scale
        )
        for n in range(3)
    ]
    for f in range(frames):
        values = upstream[f].astype(jnp.float32) * silu_slope(pre_three[f])
        wides[0][f, 1 : rows + 1] = values.astype(jnp.bfloat16)
    gathered()
    halos[0][1]()
    for each in halos:
        each[0]()

    for n in range(3):
        _, _, corners, arrive_block, arrive_corners, _ = halos[n]
        if n > 0:
            kernel_term(turned, shifted, terms[n - 1])
            sums[n - 1][0]()
        loads[n].wait()
        loads[3 + n].wait()
        for a, b in TAPS:
            for c in range(3):
                flipped[a * 3 + b, c * channels : (c + 1) * channels] = kernels[n][a, b, c].T
        for f in range(frames):
            shift(wides[n], shifted, f, 1, rows)
        back(shifted, flipped, totals, False, False)
        for f in range(frames):
            values = saved[n][f].reshape(size, channels)
            if n < 2:
                slopes[f] = silu_slope(values)
                wide = values.astype(jnp.float32)
                values = (wide * jax.nn.sigmoid(wide)).astype(jnp.bfloat16)
            turned[f] = values.T
        corners()
        if n > 0:
            sums[n - 1][1]()
        if n > 1:
            sums[n - 2][3]()
        for f in range(frames):
            shift(wides[n], shifted, f, 0, 1)
            shift(wides[n], shifted, f, rows + 1, 1)
        back(shifted, flipped, totals, False, True)
        arrive_block()
        for f in range(frames, frames + 2):
            shift(wides[n], shifted, f, 1, rows)
        back(shifted, flipped, totals, True, False)
        if n == 2:
            kernel_term(turned, shifted, terms[n], (2,))
        arrive_corners()
        if n > 0:
            sums[n - 1][2]()
        for f in range(frames, frames + 2):
            shift(wides[n], shifted, f, 0, 1)
            shift(wides[n], shifted, f, rows + 1, 1)
        if n == 2:
            kernel_term(turned, shifted, terms[n], (0, 1))
            sums[n][0]()
            sums[n - 2][4]()
        back(shifted, flipped, totals, True, True)
        for f in range(frames):
            if n < 2:
                total = totals[f] * slopes[f]
                wides[n + 1][f, 1 : rows + 1] = total.astype(jnp.bfloat16).reshape(
                    rows, cols, channels
                )
            else:
                total = totals[f].astype(jnp.bfloat16)
                input_gradient[f] = total.reshape(rows, cols, channels)
        if n < 2:
            halos[n + 1][1]()
    for n, stage in (
        (2, 1), (2, 2), (1, 3), (0, 5), (2, 3), (1, 4), (2, 4), (1, 5), (2, 5), (0, 6), (1, 6), (2, 6)
    ):
        sums[n][stage]()
    for halo in halos:
        halo[5]()


def shards(
    layer_input, pre_one, pre_two, pre_three, kernel_one, kernel_two, kernel_three, upstream
):
    frames, rows, cols, channels = layer_input.shape
    ta_n, ha_n = lax.axis_size("ta"), lax.axis_size("ha")
    scale = 1.0 / math.sqrt(frames * rows * cols * ta_n * ha_n)
    piece = channels // ha_n
    term_shape = (ha_n // 2, 2, 2, 2, 7, piece, channels)
    sems = reduce_sems(ha_n // 2)
    anywhere = pl.BlockSpec(memory_space=pl.ANY)
    half = jnp.bfloat16
    scratch = (
        [pltpu.VMEM(layer_input.shape, half)] * 3
        + [pltpu.VMEM(kernel_one.shape, half)] * 3
        + [pltpu.VMEM((frames + 2, rows + 2, cols, channels), half)] * 3
        + [pltpu.VMEM(term_shape, half)] * 3
        + [
            pltpu.VMEM((frames + 2, rows + 2, cols, 3 * channels), half),
            pltpu.VMEM((9, 3 * channels, channels), half),
            pltpu.VMEM((frames, channels, rows * cols), half),
            pltpu.VMEM((frames, rows * cols, channels), jnp.float32),
            pltpu.VMEM((frames, rows * cols, channels), jnp.float32),
        ]
        + reduce_shapes(term_shape) * 3
        + [
            pltpu.SemaphoreType.DMA((6,)),
            pltpu.SemaphoreType.DMA((3, 1 + 4 * frames)),
            pltpu.SemaphoreType.DMA((3, 1 + 4 * frames)),
            pltpu.SemaphoreType.DMA((3, sems)),
            pltpu.SemaphoreType.DMA((3, sems)),
        ]
    )
    result = pl.pallas_call(
        functools.partial(whole_kernel, ta_n, ha_n, scale),
        out_shape=[jax.ShapeDtypeStruct(layer_input.shape, half)]
        + [jax.ShapeDtypeStruct((27, piece, channels), jnp.float32)] * 3,
        in_specs=[VMEM] * 2 + [anywhere] * 6,
        out_specs=[VMEM] * 4,
        scratch_shapes=scratch,
        compiler_params=pltpu.CompilerParams(
            collective_id=0, has_side_effects=True, vmem_limit_bytes=56 * 1024 * 1024
        ),
        name="backward",
    )(upstream, pre_three, pre_two, pre_one, layer_input, kernel_three, kernel_two, kernel_one)
    input_gradient, *sums = result
    three, two, one = [total.reshape(3, 3, 3, piece, channels) for total in sums]
    return (input_gradient, one, two, three)


def solution(mesh):
    return jax.shard_map(
        shards,
        mesh=mesh,
        in_specs=(
            P("ta", "ha", None, None),
            P("ta", "ha", None, None),
            P("ta", "ha", None, None),
            P("ta", "ha", None, None),
            P(),
            P(),
            P(),
            P("ta", "ha", None, None),
        ),
        out_specs=(
            P("ta", "ha", None, None),
            P(None, None, None, "ha", None),
            P(None, None, None, "ha", None),
            P(None, None, None, "ha", None),
        ),
        check_vma=False,
    )
```

```python
import functools
import math

import jax
import jax.numpy as jnp
from jax import lax
from jax.experimental import pallas as pl
from jax.experimental.pallas import tpu as pltpu
from jax.sharding import PartitionSpec as P

MESH = pl.DeviceIdType.MESH
VMEM = pl.BlockSpec(memory_space=pltpu.VMEM)


def silu_slope(pre_values):
    values = pre_values.astype(jnp.float32)
    sigmoid = jax.nn.sigmoid(values)
    return sigmoid * (1.0 + values * (1.0 - sigmoid))


def halo_stages(ta_n, ha_n, wide, send_sems, recv_sems):
    ta, ha = lax.axis_index("ta"), lax.axis_index("ha")
    frames, rows = wide.shape[0] - 2, wide.shape[1] - 2
    has_up, has_down = ha > 0, ha < ha_n - 1
    has_earlier, has_later = ta > 0, ta < ta_n - 1

    def copy(index, source, target, d_ta, d_ha):
        return pltpu.make_async_remote_copy(
            src_ref=source,
            dst_ref=target,
            send_sem=send_sems.at[index],
            recv_sem=recv_sems.at[index],
            device_id=(ha + d_ha, ta + d_ta),
            device_id_type=MESH,
        )

    now, ahead = pl.ds(0, frames), pl.ds(frames, 2)
    each = range(frames)
    below = [copy(1 + 4 * f, wide.at[f, rows], wide.at[f, 0], 0, 1) for f in each]
    above = [copy(2 + 4 * f, wide.at[f, 1], wide.at[f, rows + 1], 0, -1) for f in each]
    earlier = copy(0, wide.at[now, pl.ds(1, rows)], wide.at[ahead, pl.ds(1, rows)], -1, 0)
    corner_top = [copy(3 + 4 * f, wide.at[f, 0], wide.at[frames + f, 0], -1, 0) for f in each]
    corner_end = [
        copy(4 + 4 * f, wide.at[f, rows + 1], wide.at[frames + f, rows + 1], -1, 0) for f in each
    ]

    def clear():
        zero_row = jnp.zeros((frames,) + wide.shape[2:], wide.dtype)

        @pl.when(jnp.logical_not(has_up))
        def _():
            wide[0:frames, 0] = zero_row
            wide[frames : frames + 2, 0] = zero_row

        @pl.when(jnp.logical_not(has_down))
        def _():
            wide[0:frames, rows + 1] = zero_row
            wide[frames : frames + 2, rows + 1] = zero_row

        @pl.when(jnp.logical_not(has_later))
        def _():
            for row in range(rows + 2):
                wide[frames : frames + 2, row] = zero_row

    def start():
        for f in each:
            pl.when(has_down)(below[f].start)
            pl.when(has_up)(above[f].start)
        pl.when(has_earlier)(earlier.start)

    def corners():
        for f in each:

            @pl.when(has_up)
            def _():
                below[f].wait_recv()
                pl.when(has_earlier)(corner_top[f].start)

            @pl.when(has_down)
            def _():
                above[f].wait_recv()
                pl.when(has_earlier)(corner_end[f].start)

    def arrive_block():
        pl.when(has_later)(earlier.wait_recv)

    def arrive_corners():
        @pl.when(has_later)
        def _():
            for f in each:
                pl.when(has_up)(corner_top[f].wait_recv)
                pl.when(has_down)(corner_end[f].wait_recv)

    def finish():
        for f in each:
            pl.when(has_down)(below[f].wait_send)
            pl.when(has_up)(above[f].wait_send)

        @pl.when(has_earlier)
        def _():
            earlier.wait_send()
            for f in each:
                pl.when(has_up)(corner_top[f].wait_send)
                pl.when(has_down)(corner_end[f].wait_send)

    return clear, start, corners, arrive_block, arrive_corners, finish


def shift(wide, shifted, f, first, count):
    cols, channels = wide.shape[2:]
    size = count * cols
    column = lax.broadcasted_iota(jnp.int32, (count, cols, channels), 1).reshape(size, channels)
    lines = wide[f, first : first + count]
    flat = lines.reshape(size, channels).astype(jnp.float32)
    after = jnp.where(column < cols - 1, pltpu.roll(flat, size - 1, 0), 0.0)
    before = jnp.where(column > 0, pltpu.roll(flat, 1, 0), 0.0)
    for place, values in ((0, after.astype(lines.dtype)), (2, before.astype(lines.dtype))):
        shifted[f, first : first + count, :, place * channels : (place + 1) * channels] = (
            values.reshape(lines.shape)
        )
    shifted[f, first : first + count, :, channels : 2 * channels] = lines


TAPS = [(a, b) for a in range(3) for b in range(3)]


def window(shifted, f, a, b):
    rows, cols, width = shifted.shape[1] - 2, shifted.shape[2], shifted.shape[3]
    return shifted[f + 2 - a, 2 - b : 2 - b + rows].reshape(rows * cols, width)


def kernel_term(turned, shifted, term, steps=(0, 1, 2)):
    channels = turned.shape[1]
    pieces = term.shape[:2] + term.shape[5:]
    term[:, :, 1, 1, 6] = jnp.zeros(pieces, term.dtype)
    for a, b in TAPS:
        if a not in steps:
            continue
        total = None
        for f in range(turned.shape[0]):
            part = jnp.dot(turned[f], window(shifted, f, a, b), preferred_element_type=jnp.float32)
            total = part if total is None else total + part
        for c in range(3):
            block = total[:, c * channels : (c + 1) * channels].astype(term.dtype)
            tap = (a * 3 + b) * 3 + c
            term[:, :, tap // 14, tap // 7 % 2, tap % 7] = block.reshape(pieces)


def back(shifted, flipped, sums, ahead, side):
    frames = sums.shape[0]
    for f in range(frames):
        total = None
        for a, b in TAPS:
            if (f + 2 - a >= frames) != ahead or (b != 1) != side:
                continue
            part = jnp.dot(
                window(shifted, f, a, b), flipped[a * 3 + b], preferred_element_type=jnp.float32
            )
            total = part if total is None else total + part
        if ahead or side:
            total = sums[f] + total
        sums[f] = total


def added(one, two):
    return (one.astype(jnp.float32) + two.astype(jnp.float32)).astype(jnp.bfloat16)


def reduce_shapes(term_shape):
    depth, tail = term_shape[0], term_shape[4:]
    half = depth // 2
    shapes = [
        (depth, 2, 2) + tail,
        (depth, 2, 2) + tail,
        (half, 2) + tail,
        (half, 2) + tail,
        (half,) + tail,
        (half, 2) + tail,
        (half, 2) + tail,
        (half,) + tail,
        (depth,) + tail,
        (depth - 1,) + tail,
        (4,) + tail,
    ]
    return [pltpu.VMEM(shape, jnp.bfloat16) for shape in shapes]


def reduce_sems(depth):
    return 5 + depth - 1 + 3


def reduce_peers(depth):
    ta, ha = lax.axis_index("ta"), lax.axis_index("ha")
    z, x, y, core = ha // 2, ha % 2, ta // 2, ta % 2
    across_core = (ha, y * 2 + 1 - core)
    across_y = (ha, (1 - y) * 2 + core)
    across_x = (z * 2 + 1 - x, ta)
    along_z = [((z + step) % depth * 2 + x, ta) for step in range(1, depth)]
    around = [(ha, (ta + step) % 4) for step in range(1, 4)]
    return across_core, across_y, across_x, along_z, around


def reduce_phases(term, out_ref, buffers, send_sems, recv_sems, scale):
    depth = term.shape[0]
    half = depth // 2
    ta, ha = lax.axis_index("ta"), lax.axis_index("ha")
    z, x, y, core = ha // 2, ha % 2, ta // 2, ta % 2
    across_core, across_y, across_x, along_z, around = reduce_peers(depth)
    from_core, cores, low_x, low, low_y, top_y, top, top_x, rest, from_z, whole = buffers

    def copy(index, source, target, peer):
        return pltpu.make_async_remote_copy(
            src_ref=source,
            dst_ref=target,
            send_sem=send_sems.at[index],
            recv_sem=recv_sems.at[index],
            device_id=peer,
            device_id_type=MESH,
        )

    core_copy = copy(0, term.at[:, :, :, 1 - core], from_core, across_core)
    low_x_copy = copy(1, cores.at[pl.ds(0, half), 1 - x], low_x, across_x)
    low_y_copy = copy(2, low.at[:, 1 - y], low_y, across_y)
    top_y_copy = copy(3, cores.at[pl.ds(half, half), :, 1 - y], top_y, across_y)
    top_x_copy = copy(4, top.at[:, 1 - x], top_x, across_x)
    z_copies = [
        copy(5 + step, rest.at[(z + step + 1) % depth], from_z.at[step], along_z[step])
        for step in range(depth - 1)
    ]
    last_copies = [
        copy(4 + depth + step, whole.at[ta], whole.at[ta], around[step]) for step in range(3)
    ]

    def start():
        core_copy.start()

    def first():
        core_copy.wait_recv()
        for row in range(half):
            cores[row] = added(term[row, :, :, core], from_core[row])
        low_x_copy.start()

    def first_y():
        for row in range(half, depth):
            cores[row] = added(term[row, :, :, core], from_core[row])
        top_y_copy.start()

    def second():
        low_x_copy.wait_recv()
        low[...] = added(cores[0:half, x], low_x[...])
        low_y_copy.start()
        top_y_copy.wait_recv()
        top[...] = added(cores[half:depth, :, y], top_y[...])
        top_x_copy.start()

    def third():
        low_y_copy.wait_recv()
        rest[0:half] = added(low[:, y], low_y[...])
        top_x_copy.wait_recv()
        rest[half:depth] = added(top[:, x], top_x[...])
        for each in z_copies:
            each.start()

    def fourth():
        total = rest[z].astype(jnp.float32)
        for step in range(depth - 1):
            z_copies[step].wait_recv()
            total = total + from_z[step].astype(jnp.float32)
        whole[ta] = total.astype(jnp.bfloat16)
        for each in last_copies:
            each.start()

    def finish():
        for each in last_copies:
            each.wait_recv()
        for tap in range(27):
            out_ref[tap] = whole[tap // 7, tap % 7].astype(jnp.float32) * scale
        for each in [core_copy, low_x_copy, low_y_copy, top_y_copy, top_x_copy] + z_copies + last_copies:
            each.wait_send()

    return start, first, first_y, second, third, fourth, finish


def greet(ha_n):
    barrier = pltpu.get_barrier_semaphore()
    ta, ha = lax.axis_index("ta"), lax.axis_index("ha")
    _, _, across_x, along_z, around = reduce_peers(ha_n // 2)
    peers = [across_x] + along_z + around
    for peer in peers:
        pl.semaphore_signal(barrier, inc=1, device_id=peer, device_id_type=MESH)
    other = ha - 1 + ha % 2 * 2
    exists = jnp.logical_and(other >= 0, other < ha_n)

    @pl.when(exists)
    def _():
        pl.semaphore_signal(barrier, inc=1, device_id=(other, ta), device_id_type=MESH)

    return lambda: pl.semaphore_wait(barrier, len(peers) + exists.astype(jnp.int32))


def whole_kernel(ta_n, ha_n, scale, *refs):
    upstream, pre_three, saved_hbm, kernels_hbm = refs[0], refs[1], refs[2:5], refs[5:8]
    input_gradient, outs = refs[8], refs[9:12]
    saved, kernels, wides, terms = refs[12:15], refs[15:18], refs[18:21], refs[21:24]
    shifted, flipped, turned, slopes, totals = refs[24:29]
    load_sems, halo_send, halo_recv, send_sems, recv_sems = refs[-5:]
    buffers = refs[29:-5]
    each = len(buffers) // 3
    frames, rows, cols, channels = upstream.shape
    size = rows * cols
    gathered = greet(ha_n)

    loads = [
        pltpu.make_async_copy(source, target, load_sems.at[n])
        for n, (source, target) in enumerate(
            zip(tuple(saved_hbm) + tuple(kernels_hbm), tuple(saved) + tuple(kernels))
        )
    ]
    for n in (0, 3, 1, 4, 2, 5):
        loads[n].start()
    halos = [
        halo_stages(ta_n, ha_n, wides[n], halo_send.at[n], halo_recv.at[n]) for n in range(3)
    ]
    sums = [
        reduce_phases(
            terms[n], outs[n], buffers[n * each : (n + 1) * each], send_sems.at[n], recv_sems.at[n], scale
        )
        for n in range(3)
    ]
    for f in range(frames):
        values = upstream[f].astype(jnp.float32) * silu_slope(pre_three[f])
        wides[0][f, 1 : rows + 1] = values.astype(jnp.bfloat16)
    gathered()
    halos[0][1]()
    for each in halos:
        each[0]()

    for n in range(3):
        _, _, corners, arrive_block, arrive_corners, _ = halos[n]
        if n > 0:
            kernel_term(turned, shifted, terms[n - 1])
            sums[n - 1][0]()
        loads[n].wait()
        loads[3 + n].wait()
        for a, b in TAPS:
            for c in range(3):
                flipped[a * 3 + b, c * channels : (c + 1) * channels] = kernels[n][a, b, c].T
        for f in range(frames):
            shift(wides[n], shifted, f, 1, rows)
        back(shifted, flipped, totals, False, False)
        for f in range(frames):
            values = saved[n][f].reshape(size, channels)
            if n < 2:
                slopes[f] = silu_slope(values)
                wide = values.astype(jnp.float32)
                values = (wide * jax.nn.sigmoid(wide)).astype(jnp.bfloat16)
            turned[f] = values.T
        corners()
        if n > 0:
            sums[n - 1][1]()
        if n > 1:
            sums[n - 2][3]()
        for f in range(frames):
            shift(wides[n], shifted, f, 0, 1)
            shift(wides[n], shifted, f, rows + 1, 1)
        back(shifted, flipped, totals, False, True)
        arrive_block()
        for f in range(frames, frames + 2):
            shift(wides[n], shifted, f, 1, rows)
        back(shifted, flipped, totals, True, False)
        if n == 2:
            kernel_term(turned, shifted, terms[n], (2,))
        arrive_corners()
        if n > 0:
            sums[n - 1][2]()
        for f in range(frames, frames + 2):
            shift(wides[n], shifted, f, 0, 1)
            shift(wides[n], shifted, f, rows + 1, 1)
        if n == 2:
            kernel_term(turned, shifted, terms[n], (0, 1))
            sums[n][0]()
            sums[n - 2][4]()
        back(shifted, flipped, totals, True, True)
        for f in range(frames):
            if n < 2:
                total = totals[f] * slopes[f]
                wides[n + 1][f, 1 : rows + 1] = total.astype(jnp.bfloat16).reshape(
                    rows, cols, channels
                )
            else:
                total = totals[f].astype(jnp.bfloat16)
                input_gradient[f] = total.reshape(rows, cols, channels)
        if n < 2:
            halos[n + 1][1]()
    for n, stage in (
        (2, 1), (2, 2), (1, 3), (0, 5), (2, 3), (1, 4), (2, 4), (1, 5), (2, 5), (0, 6), (1, 6), (2, 6)
    ):
        sums[n][stage]()
    for halo in halos:
        halo[5]()


def settle(*refs):
    for source, target in zip(refs[:4], refs[4:]):
        target[...] = source[...]


def shards(
    layer_input, pre_one, pre_two, pre_three, kernel_one, kernel_two, kernel_three, upstream
):
    frames, rows, cols, channels = layer_input.shape
    ta_n, ha_n = lax.axis_size("ta"), lax.axis_size("ha")
    scale = 1.0 / math.sqrt(frames * rows * cols * ta_n * ha_n)
    piece = channels // ha_n
    term_shape = (ha_n // 2, 2, 2, 2, 7, piece, channels)
    sems = reduce_sems(ha_n // 2)
    anywhere = pl.BlockSpec(memory_space=pl.ANY)
    half = jnp.bfloat16
    scratch = (
        [pltpu.VMEM(layer_input.shape, half)] * 3
        + [pltpu.VMEM(kernel_one.shape, half)] * 3
        + [pltpu.VMEM((frames + 2, rows + 2, cols, channels), half)] * 3
        + [pltpu.VMEM(term_shape, half)] * 3
        + [
            pltpu.VMEM((frames + 2, rows + 2, cols, 3 * channels), half),
            pltpu.VMEM((9, 3 * channels, channels), half),
            pltpu.VMEM((frames, channels, rows * cols), half),
            pltpu.VMEM((frames, rows * cols, channels), jnp.float32),
            pltpu.VMEM((frames, rows * cols, channels), jnp.float32),
        ]
        + reduce_shapes(term_shape) * 3
        + [
            pltpu.SemaphoreType.DMA((6,)),
            pltpu.SemaphoreType.DMA((3, 1 + 4 * frames)),
            pltpu.SemaphoreType.DMA((3, 1 + 4 * frames)),
            pltpu.SemaphoreType.DMA((3, sems)),
            pltpu.SemaphoreType.DMA((3, sems)),
        ]
    )
    result = pl.pallas_call(
        functools.partial(whole_kernel, ta_n, ha_n, scale),
        out_shape=[jax.ShapeDtypeStruct(layer_input.shape, half)]
        + [jax.ShapeDtypeStruct((27, piece, channels), jnp.float32)] * 3,
        in_specs=[VMEM] * 2 + [anywhere] * 6,
        out_specs=[VMEM] * 4,
        scratch_shapes=scratch,
        compiler_params=pltpu.CompilerParams(
            collective_id=0, has_side_effects=True, vmem_limit_bytes=56 * 1024 * 1024
        ),
        name="backward",
    )(upstream, pre_three, pre_two, pre_one, layer_input, kernel_three, kernel_two, kernel_one)
    input_gradient, *sums = pl.pallas_call(
        settle,
        out_shape=[jax.ShapeDtypeStruct(each.shape, each.dtype) for each in result],
        in_specs=[VMEM] * 4,
        out_specs=[VMEM] * 4,
        name="settle",
    )(*result)
    three, two, one = [total.reshape(3, 3, 3, piece, channels) for total in sums]
    return (input_gradient, one, two, three)


def solution(mesh):
    return jax.shard_map(
        shards,
        mesh=mesh,
        in_specs=(
            P("ta", "ha", None, None),
            P("ta", "ha", None, None),
            P("ta", "ha", None, None),
            P("ta", "ha", None, None),
            P(),
            P(),
            P(),
            P("ta", "ha", None, None),
        ),
        out_specs=(
            P("ta", "ha", None, None),
            P(None, None, None, "ha", None),
            P(None, None, None, "ha", None),
            P(None, None, None, "ha", None),
        ),
        check_vma=False,
    )
```
